128 devices in a mesh: gx: 8 (over x, core), gy: 16 (over z, y).
Axes of the slice: x: 4, y: 4, z: 4, core: 2. Of those that a mesh axis runs over, the one named last changes fastest.
Arguments:
- table: bfloat16 [65536, 512], P('gy'), may hold values from -40 to 40
- history: bfloat16 [2, 128, 1024, 512], P(None, 'gy', 'gx'), may hold values from -40 to 40
- lengths: int32 [16, 8], P('gy'), may hold values from 341 to 1024, as said below
- assignment: int32 [16, 8], P('gy'), may hold values from 0 to 7, each once within a row
- cand_owner: int32 [196608, 1], P(('gx', 'gy')), may hold values from 0 to 15; in each aligned block of 1536 rows (0 to 1535, 1536 to 3071, ...) at most 192 rows name the same one
- cand_row: int32 [196608], P(('gx', 'gy')), may hold values from 0 to 4095
- norm_gain: float32 [2, 512], replicated, may hold values from 0.1 to 1.9
- w_query: bfloat16 [2, 512, 1024], replicated, may hold values from -0.5 to 0.5
- w_key: bfloat16 [2, 512, 1024], replicated, may hold values from -1 to 1
- attn_gain: float32 [2, 512], replicated, may hold values from 0.1 to 1.9
- w_out: bfloat16 [2, 512, 512], replicated, may hold values from -0.25 to 0.25
Outputs:
- cand_out: bfloat16 [196608, 512], P(('gx', 'gy'))
The draws below stay inside these ranges and needn't reach their ends.
Inputs may be any that keep to these rules, and one draw needn't show every extreme that they name: `lengths`: some user has exactly 1024 live positions and some exactly 341. `assignment`: each row names each of its column's 8 users once. `cand_owner`: within the 1536 candidates of one device no table shard is named more than 192 times.
All inputs are finite; a program needn't handle non-finite values.
Results may differ from the reference program's by a relative error of at most 0.0075.
Values may be sent and summed in bfloat16 or wider, within the bound.
A program may use at most 128 MiB of HBM per device.

```python
import math
import jax
import jax.numpy as jnp
import numpy as np
from jax import lax

D = 512
HEADS = 4
LAYERS = 2
LMAX = 1024
CAND = 1536
ROWS = 4096
CAP = 192
VOCAB = 65536
USERS = 128
TOTAL_CAND = 196608
N_GX = 8
N_GY = 16


def scaled_field(key, array_shape):
    key_rows, key_cols, key_base = jax.random.split(key, 3)
    row_shape = array_shape[:-1] + (1,)
    col_shape = (1,) * (len(array_shape) - 1) + (array_shape[-1],)
    row_scale = jnp.exp(jax.random.uniform(key_rows, row_shape, jnp.float32, math.log(0.3), math.log(3.0)))
    col_scale = jnp.exp(jax.random.uniform(key_cols, col_shape, jnp.float32, math.log(0.3), math.log(3.0)))
    base_draw = jax.random.normal(key_base, array_shape, jnp.float32)
    return jnp.clip(base_draw * row_scale * col_scale, -40.0, 40.0).astype(jnp.bfloat16)


def draw_table(key, part):
    return scaled_field(jax.random.fold_in(key, 11), (VOCAB, D))


def draw_history(key, part):
    return scaled_field(jax.random.fold_in(key, 12), (LAYERS, USERS, LMAX, D))


def draw_lengths(key, part):
    key_values, key_order = jax.random.split(jax.random.fold_in(key, 13))
    values_all = jax.random.randint(key_values, (USERS,), LMAX // 3, LMAX + 1, dtype=jnp.int32)
    user_order = jax.random.permutation(key_order, USERS)
    values_all = values_all.at[user_order[0]].set(LMAX).at[user_order[1]].set(LMAX // 3)
    return values_all.reshape(N_GY, N_GX).astype(jnp.int32)


def draw_w_key(key, part):
    key_base = jax.random.fold_in(key, 14)
    column_ids = jnp.arange(2 * D, dtype=jnp.int32)
    column_scale = jnp.where(column_ids < D, 0.5, 0.04).astype(jnp.float32) / math.sqrt(D)
    array_shape = (LAYERS, D, 2 * D)
    base_draw = jax.random.normal(key_base, array_shape, jnp.float32)
    return jnp.clip(base_draw * column_scale[None, None, :], -1.0, 1.0).astype(jnp.bfloat16)


def place_ends(array, own_key, smallest, largest):
    longest = array.shape.index(max(array.shape))
    spots = []
    for shift in (0, 1):
        where = [jax.random.randint(jax.random.fold_in(own_key, axis), (), 0, length) for axis, length in enumerate(array.shape)]
        where[longest] = (where[longest] + shift) % array.shape[longest]
        spots.append(tuple(where))
    return array.at[spots[0]].set(smallest).at[spots[1]].set(largest)


def rank_table(count, skew):
    loads = [(1 << 20) // math.isqrt(grade ** skew) + 1 for grade in range(1, count + 1)]
    deviation = 1 + sum(loads) // (1 << 30)
    return np.cumsum(np.array([max(1, weight // deviation) for weight in loads]))


def ranked_ids(key, shape, count, skew):
    table = rank_table(count, skew)
    ticket = jax.random.randint(jax.random.fold_in(key, 1), shape, 0, int(table[count - 1]))
    grade = jnp.searchsorted(jnp.asarray(table, jnp.int32), ticket, side="right")
    return jax.random.permutation(jax.random.fold_in(key, 2), count)[grade].astype(jnp.int32)


def shared_out(rng, own, number, rows, amount, top, most, skew):
    order = jax.random.permutation(rng, amount)
    crowded, common = load_shares(amount, rows * top, most, skew, True), load_shares(amount, rows * top, most, skew, False)
    places = jnp.arange(amount)

    def named(tallies, offset_by):
        used = int((tallies > 0).sum())
        fixed = max(1, used // 4)
        passed = fixed + (places - fixed + offset_by * (used - fixed)) % max(1, amount - fixed)
        return jnp.zeros((amount,), jnp.int32).at[order[jnp.where(places < fixed, places, passed)]].set(jnp.asarray(tallies, jnp.int32))

    tallies = jnp.where(number % 4 == 0, named(crowded, number // 4), named(common, number - number // 4 - 1))
    mixed = jax.random.permutation(jax.random.fold_in(own, 3), amount)
    source_of, taker = mixed[0:amount // 2 * 2:2], mixed[1:amount // 2 * 2:2]
    margin = jnp.minimum(tallies[source_of] - 1, most - tallies[taker]) // 2
    margin = jnp.where((source_of == order[0]) | (taker == order[0]) | (tallies[taker] == 0), 0, jnp.maximum(margin, 0))
    passed = jax.random.randint(jax.random.fold_in(own, 4), (amount // 2,), 0, 1 << 20) % (margin + 1)
    tallies = tallies.at[source_of].add(-passed).at[taker].add(passed)
    items = jnp.searchsorted(jnp.cumsum(tallies), jnp.arange(rows * top), side="right").astype(jnp.int32)
    grid = items.reshape(top, rows).T
    grid = grid[jax.random.permutation(jax.random.fold_in(own, 1), rows)]
    offset_by = jax.random.randint(jax.random.fold_in(own, 2), (rows, 1), 0, top)
    return jnp.take_along_axis(grid, (jnp.arange(top)[None, :] + offset_by) % top, axis=1)


def load_shares(amount, total, most, lean, full):
    loads = [(1 << 20) // math.isqrt(standing ** lean) + 1 for standing in range(1, amount + 1)]
    largest = most if full else min(most, max(-(-total // amount), total * loads[0] // sum(loads)))
    least = 1 if total - largest >= amount - 1 else 0
    counts, rest = [largest] + [least] * (amount - 1), total - largest - least * (amount - 1)
    while rest > 0:
        candidates = [i for i in range(1, amount) if counts[i] < largest] or [i for i in range(1, amount) if counts[i] < most]
        whole, left = sum([loads[i] for i in candidates]), rest
        for i in candidates:
            addition = min(most - counts[i], max(1, left * loads[i] // whole), rest)
            counts[i] = counts[i] + addition
            rest = rest - addition
    return np.array(counts)


def bell_draw(stream_key, extent, spread, bound, held_as=jnp.bfloat16):
    return jnp.clip(spread * jax.random.normal(stream_key, extent, jnp.float32), -bound, bound).astype(held_as)


def setup_inputs(seed: int = 0) -> dict:
    keys = jax.random.split(jax.random.key(seed), 12)
    table = draw_table(jax.random.fold_in(keys[11], 71), 0)
    history = draw_history(jax.random.fold_in(keys[11], 71), 0)
    lengths = draw_lengths(jax.random.fold_in(keys[11], 71), 0)
    assignment = jax.vmap(lambda own: jax.random.permutation(own, N_GX))(jax.random.split(keys[3], N_GY)).reshape((N_GY, N_GX)).astype(jnp.int32)
    cand_owner_keys = jax.random.split(jax.random.fold_in(keys[4], 1), TOTAL_CAND // CAND)
    cand_owner_turns = jax.random.permutation(jax.random.fold_in(keys[4], 3), TOTAL_CAND // CAND)
    cand_owner = jax.vmap(lambda own, number: shared_out(jax.random.fold_in(keys[4], 2), own, number, CAND, N_GY, 1, CAP, 2))(cand_owner_keys, cand_owner_turns).reshape((TOTAL_CAND, 1))
    cand_row = place_ends(ranked_ids(keys[5], (TOTAL_CAND,), ROWS, 2), jax.random.fold_in(keys[5], 3), 0, ROWS - 1).astype(jnp.int32)
    norm_gain = jnp.clip(1.0 + 0.18 * jax.random.normal(keys[6], (LAYERS, D), jnp.float32), 0.1, 1.9)
    w_query = bell_draw(keys[7], (LAYERS, D, 2 * D), (D // 4) ** -0.5, 0.5)
    w_key = draw_w_key(jax.random.fold_in(keys[11], 71), 0)
    attn_gain = jnp.clip(1.0 + 0.18 * jax.random.normal(keys[9], (LAYERS, D), jnp.float32), 0.1, 1.9)
    w_out = bell_draw(keys[10], (LAYERS, D, D), D ** -0.5, 0.25)
    return {"table": table, "history": history, "lengths": lengths, "assignment": assignment, "cand_owner": cand_owner, "cand_row": cand_row, "norm_gain": norm_gain, "w_query": w_query, "w_key": w_key, "attn_gain": attn_gain, "w_out": w_out}


epsilon = 1e-06

def rms_scale(vector, gain_row):
    return vector * lax.rsqrt(lax.optimization_barrier(jnp.mean(vector * vector, axis=-1, keepdims=True)) + epsilon) * gain_row

def attend(query_part, key_rows, value_rows, live_mask):
    head_size = D // HEADS
    count_rows = query_part.shape[0]
    queries = query_part.astype(jnp.float32).reshape(count_rows, HEADS, head_size)
    keyed = key_rows.astype(jnp.float32).reshape(LMAX, HEADS, head_size)
    valued = value_rows.astype(jnp.float32).reshape(LMAX, HEADS, head_size)
    scores = jnp.einsum('chd,lhd->hcl', queries, keyed) * head_size ** (-0.5)
    weights = jnp.where(live_mask[None, None, :], jax.nn.silu(scores), 0.0).astype(jnp.bfloat16)
    attended = jnp.einsum('hcl,lhd->chd', weights.astype(jnp.float32), valued)
    return attended.reshape(count_rows, D)

def score_request(embedded_rows, user_history, length, norm_gain, w_query, w_key, attn_gain, w_out):
    stream = embedded_rows.astype(jnp.float32)
    live_mask = jnp.arange(LMAX, dtype=jnp.int32) < length
    for layer_index in range(LAYERS):
        normed = rms_scale(stream, norm_gain[layer_index]).astype(jnp.bfloat16)
        gate_query = jax.nn.silu(jnp.dot(normed, w_query[layer_index], preferred_element_type=jnp.float32)).astype(jnp.bfloat16)
        history_normed = rms_scale(user_history[layer_index].astype(jnp.float32), norm_gain[layer_index]).astype(jnp.bfloat16)
        key_value = jax.nn.silu(jnp.dot(history_normed, w_key[layer_index], preferred_element_type=jnp.float32)).astype(jnp.bfloat16)
        attended = attend(gate_query[:, D:], key_value[:, :D], key_value[:, D:], live_mask)
        gated_out = (rms_scale(attended, attn_gain[layer_index]) * gate_query[:, :D].astype(jnp.float32)).astype(jnp.bfloat16)
        stream = stream + jnp.dot(gated_out, w_out[layer_index], preferred_element_type=jnp.float32)
    return stream.astype(jnp.bfloat16)

def reference(table, history, lengths, assignment, cand_owner, cand_row, norm_gain, w_query, w_key, attn_gain, w_out):
    global_rows = (cand_owner[:, 0] * ROWS + cand_row).astype(jnp.int32)
    embedded = jnp.take(table, global_rows, axis=0).reshape(N_GX * N_GY, CAND, D)
    device_ids = jnp.arange(N_GX * N_GY, dtype=jnp.int32)
    across = device_ids // N_GY
    column = device_ids % N_GY
    slot_index = assignment[column, across].astype(jnp.int32)
    user_index = (column * N_GX + slot_index).astype(jnp.int32)
    live_length = lengths[column, slot_index].astype(jnp.int32)

    def one_device(packed):
        embedded_rows, who, length = packed
        user_history = lax.dynamic_index_in_dim(history, who, axis=1, keepdims=False)
        return score_request(embedded_rows, user_history, length, norm_gain, w_query, w_key, attn_gain, w_out)
    scored = lax.map(one_device, (embedded, user_index, live_length))
    return scored.reshape(N_GX * N_GY * CAND, D)
```

```python
import functools

import jax
import jax.numpy as jnp
from jax import lax
from jax.experimental import pallas as pl
from jax.experimental.pallas import tpu as pltpu
from jax.sharding import PartitionSpec as P

HEADS = 4
LAYERS = 2
EPSILON = 1e-06
MESH = pl.DeviceIdType.MESH
f32, bf16, i32 = jnp.float32, jnp.bfloat16, jnp.int32

OFFSETS = (
    (2, 2), (1, 0), (2, 1), (0, 3), (1, 2), (3, 0), (2, 3), (0, 1),
    (3, 2), (1, 1), (0, 2), (3, 3), (2, 0), (1, 3), (3, 1),
)
SIDE = 4
PEERS = len(OFFSETS)
PACKED_Z = sum(z * SIDE**k for k, (z, _) in enumerate(OFFSETS))
PACKED_Y = sum(y * SIDE**k for k, (_, y) in enumerate(OFFSETS))


def silu(v):
    half = v * 0.5
    return half + half * jnp.tanh(half)


def rms_scale(vector, gain_row):
    return vector * lax.rsqrt(jnp.mean(vector * vector, axis=-1, keepdims=True) + EPSILON) * gain_row


def bucket_kernel(capacity, owner_ref, row_ref, slot_ref, request_ref, square):
    blocks = owner_ref.shape[0]
    groups = request_ref.shape[0]
    lane = lax.broadcasted_iota(i32, (128, 128), 1)
    below = (lane < lax.broadcasted_iota(i32, (128, 128), 0)).astype(bf16)
    slot_lane = lax.broadcasted_iota(i32, (128, 2 * 128), 1).astype(f32)
    owner_lane = (lane % groups).astype(f32)
    square[...] = jnp.zeros_like(square)
    square[0:blocks, :] = owner_ref[...].astype(f32)
    owners = square[...].T
    square[0:blocks, :] = (row_ref[...] // 64).astype(f32)
    high = square[...].T
    square[0:blocks, :] = (row_ref[...] % 64).astype(f32)
    low = square[...].T
    carry = jnp.zeros((1, 128), f32)
    parts = jnp.zeros((128, 2 * 128), f32)
    for b in range(blocks):
        owner = owners[:, b : b + 1]
        named = owner == owner_lane
        onehot = jnp.where(named & (lane < groups), 1.0, 0.0)
        prior = jnp.dot(below, onehot.astype(bf16), preferred_element_type=f32) + carry
        carry = carry + jnp.sum(onehot, axis=0, keepdims=True)
        rank = jnp.sum(onehot * prior, axis=1, keepdims=True)
        slot_ref[b * 128 : (b + 1) * 128, :] = jnp.broadcast_to(
            owner * capacity + rank, (128, 128)
        ).astype(i32)
        digits = jnp.where(lane < groups, high[:, b : b + 1], low[:, b : b + 1])
        digits = jnp.where(named & (lane < 2 * groups), digits, 0.0)
        chosen = jnp.where(rank == slot_lane, 1.0, 0.0)
        parts = parts + jnp.dot(
            digits.T.astype(bf16), chosen.astype(bf16), preferred_element_type=f32
        )
    rows = (parts[0:groups] * 64.0 + parts[groups : 2 * groups]).astype(i32)
    request_ref[:, 0, :] = rows[:, 0:128]
    request_ref[:, 1, :] = rows[:, 128:256]


def exchange_kernel(
    capacity,
    request_ref,
    slot_ref,
    gain_ref,
    assign_ref,
    length_ref,
    table_hbm,
    history_hbm,
    w_key_hbm,
    stream_ref,
    kv_ref,
    table_in,
    table,
    asked,
    asked_scalar,
    stage,
    outbox,
    inbox,
    total,
    history_in,
    history_out,
    history_all,
    w_key,
    local_sem,
    asked_send,
    asked_recv,
    row_send,
    row_recv,
    hist_send,
    hist_recv,
):
    count = stream_ref.shape[0]
    width = stream_ref.shape[1]
    members = lax.axis_size("gx")
    span = history_in.shape[2]
    gx = lax.axis_index("gx")
    gy = lax.axis_index("gy")
    my_z, my_y = gy // SIDE, gy % SIDE

    def peer(dz, dy):
        return ((my_z + dz + SIDE) % SIDE) * SIDE + (my_y + dy + SIDE) % SIDE

    table_copy = pltpu.make_async_copy(table_hbm, table_in, local_sem.at[0])
    history_copy = pltpu.make_async_copy(history_hbm, history_in, local_sem.at[1])
    weight_copy = pltpu.make_async_copy(w_key_hbm, w_key, local_sem.at[2])
    history_copy.start()
    table_copy.start()
    weight_copy.start()

    barrier = pltpu.get_barrier_semaphore()
    for dz, dy in OFFSETS:
        pl.semaphore_signal(barrier, inc=1, device_id=(gx, peer(dz, dy)), device_id_type=MESH)
    for d in range(1, members):
        pl.semaphore_signal(
            barrier, inc=1, device_id=((gx + d) % members, gy), device_id_type=MESH
        )
    pl.semaphore_wait(barrier, PEERS + members - 1)

    ask = []
    for k, (dz, dy) in enumerate(OFFSETS):
        to = peer(dz, dy)
        ask.append(
            pltpu.make_async_remote_copy(
                request_ref.at[to],
                asked.at[k],
                asked_send.at[k],
                asked_recv.at[k],
                device_id=(gx, to),
                device_id_type=MESH,
            )
        )
        ask[-1].start()

    history_copy.wait()
    for l in range(LAYERS):
        for d in range(1, members):
            to = (gx + d) % members
            history_out[l, d] = history_in[l, assign_ref[0, to]]
        here = pl.ds(pl.multiple_of(gx * span, span), span)
        history_all[l, here, :] = history_in[l, assign_ref[0, gx]]
    spread = []
    for l in range(LAYERS):
        for d in range(1, members):
            to = (gx + d) % members
            spread.append(
                pltpu.make_async_remote_copy(
                    history_out.at[l, d],
                    history_all.at[l, pl.ds(pl.multiple_of(gx * span, span), span), :],
                    hist_send.at[l, d],
                    hist_recv.at[l, d],
                    device_id=(to, gy),
                    device_id_type=MESH,
                )
            )
            spread[-1].start()

    table_copy.wait()
    step = 256

    @pl.loop(0, table_in.shape[0] // step)
    def _(t):
        at = pl.ds(pl.multiple_of(t * step, step), step)
        for c in range(width // 128):
            table[at, c, :] = table_in[at, c * 128 : (c + 1) * 128].astype(f32)

    def collect(index, box, slot):
        @pl.loop(0, capacity // 16)
        def _(t):
            for j in range(16):
                place = t * 16 + j
                row = asked_scalar[index, place // 128, place % 128]
                stage[pl.ds(place, 1)] = table[pl.ds(row, 1)]

        for c in range(width // 128):
            box[slot, :, c * 128 : (c + 1) * 128] = stage[:, c, :].astype(bf16)

    asked[PEERS] = request_ref[gy]
    for k in range(PEERS):
        ask[k].wait_recv()
    scalars = pltpu.make_async_copy(asked, asked_scalar, local_sem.at[3])
    scalars.start()
    scalars.wait()

    def reply(k, dz, dy):
        to = peer(-dz, -dy)
        return pltpu.make_async_remote_copy(
            outbox.at[k],
            inbox.at[k + 1],
            row_send.at[k],
            row_recv.at[k],
            device_id=(gx, to),
            device_id_type=MESH,
        )

    def serve(k, digits):
        z, y, last_z, last_y = digits
        collect(k, outbox, k)

        @pl.when(k > 0)
        def _():
            reply(k - 1, last_z, last_y).start()

        return z // SIDE, y // SIDE, z % SIDE, y % SIDE

    lax.fori_loop(0, PEERS, serve, (PACKED_Z, PACKED_Y, 0, 0))
    reply(PEERS - 1, *OFFSETS[-1]).start()
    collect(PEERS, inbox, 0)

    half = count // 2
    lane = lax.broadcasted_iota(i32, (1, 4 * capacity), 1)

    def place(first):
        target = jnp.zeros((1, 4 * capacity), i32)
        for j in range(4):
            slot = first + j
            if slot == 0:
                owner = gy
            else:
                owner = peer(*OFFSETS[slot - 1])
                reply(slot - 1, *OFFSETS[slot - 1]).wait_recv()
            target = jnp.where(lane // capacity == j, lane - j * capacity + owner * capacity, target)
        rows = inbox[first : first + 4].reshape(4 * capacity, width)

        @pl.loop(0, 2)
        def _(b):
            at = pl.ds(pl.multiple_of(b * half, half), half)
            slots = slot_ref[at, :]
            onehot = jnp.concatenate(
                [
                    jnp.where(slots == target[:, c : c + 128], 1.0, 0.0).astype(bf16)
                    for c in range(0, 4 * capacity, 128)
                ],
                axis=1,
            )
            found = jnp.dot(onehot, rows, preferred_element_type=f32)
            if first == 0:
                total[at, :] = found
            elif first == 12:
                stream_ref[at, :] = (total[at, :] + found).astype(bf16)
            else:
                total[at, :] = total[at, :] + found

    live = length_ref[0, assign_ref[0, gx]]

    def project(l):
        for d in range(1, members):
            spread[l * (members - 1) + d - 1].wait_recv()
        size = 512

        @pl.loop(0, history_all.shape[1] // size)
        def _(b):
            at = pl.ds(pl.multiple_of(b * size, size), size)
            normed = rms_scale(history_all[l, at, :].astype(f32), gain_ref[l : l + 1, :])
            both = silu(jnp.dot(normed.astype(bf16), w_key[l], preferred_element_type=f32))
            position = lax.broadcasted_iota(i32, (size, 1), 0) + b * size
            kv_ref[l, at, 0:width] = both[:, 0:width].astype(bf16)
            kv_ref[l, at, width : 2 * width] = jnp.where(
                position < live, both[:, width : 2 * width], 0.0
            ).astype(bf16)

    weight_copy.wait()
    place(0)
    project(0)
    place(4)
    project(1)
    place(8)
    place(12)
    for k in range(PEERS):
        ask[k].wait_send()
        reply(k, *OFFSETS[k]).wait_send()
    for copy in spread:
        copy.wait_send()


def layers_kernel(emb_ref, kv_ref, wq_ref, wo_ref, gain_ref, attn_ref, out_ref):
    width = emb_ref.shape[1]
    head = width // HEADS
    length = kv_ref.shape[1]
    keys = 256
    stream = emb_ref[...].astype(f32)
    for l in range(LAYERS):
        normed = rms_scale(stream, gain_ref[l : l + 1, :]).astype(bf16)
        gate_query = silu(jnp.dot(normed, wq_ref[l], preferred_element_type=f32)).astype(bf16)
        outs = []
        for h in range(HEADS):
            query = gate_query[:, width + h * head : width + (h + 1) * head]
            total = None
            for k in range(0, length, keys):
                scores = lax.dot_general(
                    query,
                    kv_ref[l, k : k + keys, h * head : (h + 1) * head],
                    (((1,), (1,)), ((), ())),
                    preferred_element_type=f32,
                )
                weights = silu(scores * head**-0.5).astype(bf16)
                part = jnp.dot(
                    weights,
                    kv_ref[l, k : k + keys, width + h * head : width + (h + 1) * head],
                    preferred_element_type=f32,
                )
                total = part if total is None else total + part
            outs.append(total)
        attended = jnp.concatenate(outs, axis=1)
        gated = rms_scale(attended, attn_ref[l : l + 1, :]) * gate_query[:, :width].astype(f32)
        stream = stream + jnp.dot(gated.astype(bf16), wo_ref[l], preferred_element_type=f32)
    out_ref[...] = stream.astype(bf16)


VMEM = pl.BlockSpec(memory_space=pltpu.VMEM)
SMEM = pl.BlockSpec(memory_space=pltpu.SMEM)
ANY = pl.BlockSpec(memory_space=pl.ANY)


def local(
    table,
    history,
    lengths,
    assignment,
    cand_owner,
    cand_row,
    norm_gain,
    w_query,
    w_key,
    attn_gain,
    w_out,
):
    groups = lax.axis_size("gy")
    members = lax.axis_size("gx")
    count = cand_row.shape[0]
    rows, width = table.shape
    span = history.shape[2]
    capacity = 2 * count // groups
    slots, requests = pl.pallas_call(
        functools.partial(bucket_kernel, capacity),
        out_shape=(
            jax.ShapeDtypeStruct((count, 128), i32),
            jax.ShapeDtypeStruct((groups, 2, 128), i32),
        ),
        in_specs=[VMEM, VMEM],
        out_specs=(VMEM, VMEM),
        scratch_shapes=[pltpu.VMEM((128, 128), f32)],
        name="bucket",
    )(cand_owner.reshape(count // 128, 128), cand_row.reshape(count // 128, 128))
    dma = pltpu.SemaphoreType.DMA
    stream, key_value = pl.pallas_call(
        functools.partial(exchange_kernel, capacity),
        out_shape=(
            jax.ShapeDtypeStruct((count, width), bf16),
            jax.ShapeDtypeStruct((LAYERS, span * members, 2 * width), bf16),
        ),
        in_specs=[VMEM, VMEM, VMEM, SMEM, SMEM, ANY, ANY, ANY],
        out_specs=(VMEM, VMEM),
        scratch_shapes=[
            pltpu.VMEM((rows, width), bf16),
            pltpu.VMEM((rows, width // 128, 128), f32),
            pltpu.VMEM((groups, 2, 128), i32),
            pltpu.SMEM((groups, 2, 128), i32),
            pltpu.VMEM((capacity, width // 128, 128), f32),
            pltpu.VMEM((PEERS, capacity, width), bf16),
            pltpu.VMEM((groups, capacity, width), bf16),
            pltpu.VMEM((count, width), f32),
            pltpu.VMEM(history.shape, bf16),
            pltpu.VMEM((LAYERS, members, span, width), bf16),
            pltpu.VMEM((LAYERS, members * span, width), bf16),
            pltpu.VMEM(w_key.shape, bf16),
            dma((4,)),
            dma((PEERS,)),
            dma((PEERS,)),
            dma((PEERS,)),
            dma((PEERS,)),
            dma((LAYERS, members)),
            dma((LAYERS, members)),
        ],
        compiler_params=pltpu.CompilerParams(
            collective_id=0, has_side_effects=True, vmem_limit_bytes=60 << 20
        ),
        name="exchange",
    )(requests, slots, norm_gain, assignment, lengths, table, history, w_key)
    block = count // 2
    return pl.pallas_call(
        layers_kernel,
        grid=(count // block,),
        out_shape=jax.ShapeDtypeStruct((count, width), bf16),
        in_specs=[pl.BlockSpec((block, width), lambda i: (i, 0)), VMEM, VMEM, VMEM, VMEM, VMEM],
        out_specs=pl.BlockSpec((block, width), lambda i: (i, 0)),
        compiler_params=pltpu.CompilerParams(vmem_limit_bytes=60 << 20),
        name="layers",
    )(stream, key_value, w_query, w_out, norm_gain, attn_gain)


def solution(mesh):
    both = ("gx", "gy")
    return jax.shard_map(
        local,
        mesh=mesh,
        in_specs=(
            P("gy", None),
            P(None, "gy", "gx", None),
            P("gy", None),
            P("gy", None),
            P(both, None),
            P(both),
            P(),
            P(),
            P(),
            P(),
            P(),
        ),
        out_specs=P(both, None),
        check_vma=False,
    )
```

```python
import functools

import jax
import jax.numpy as jnp
from jax import lax
from jax.experimental import pallas as pl
from jax.experimental.pallas import tpu as pltpu
from jax.sharding import PartitionSpec as P

HEADS = 4
LAYERS = 2
EPSILON = 1e-06
MESH = pl.DeviceIdType.MESH
f32, bf16, i32 = jnp.float32, jnp.bfloat16, jnp.int32

OFFSETS = (
    (2, 2), (1, 0), (2, 1), (0, 3), (1, 2), (3, 0), (2, 3), (0, 1),
    (3, 2), (1, 1), (0, 2), (3, 3), (2, 0), (1, 3), (3, 1),
)
SIDE = 4
PEERS = len(OFFSETS)
PACKED_Z = sum(z * SIDE**k for k, (z, _) in enumerate(OFFSETS))
PACKED_Y = sum(y * SIDE**k for k, (_, y) in enumerate(OFFSETS))


def silu(v):
    half = v * 0.5
    return half + half * jnp.tanh(half)


def rms_scale(vector, gain_row):
    return vector * lax.rsqrt(jnp.mean(vector * vector, axis=-1, keepdims=True) + EPSILON) * gain_row


def program_kernel(
    capacity,
    owner_ref,
    row_ref,
    gain_ref,
    attn_ref,
    assign_ref,
    length_ref,
    table_hbm,
    history_hbm,
    w_key_hbm,
    w_query_hbm,
    w_out_hbm,
    out_ref,
    square,
    counts,
    counts_scalar,
    rank_ref,
    table_in,
    table,
    request,
    asked,
    asked_scalar,
    stage,
    outbox,
    inbox,
    taken,
    total,
    history_in,
    history_out,
    history_all,
    key_value,
    w_key,
    w_query,
    w_out,
    local_sem,
    asked_send,
    asked_recv,
    row_send,
    row_recv,
    hist_send,
    hist_recv,
):
    count, width = out_ref.shape
    half = count // 2
    blocks = count // 128
    groups = lax.axis_size("gy")
    members = lax.axis_size("gx")
    span = history_in.shape[2]
    gx = lax.axis_index("gx")
    gy = lax.axis_index("gy")
    my_z, my_y = gy // SIDE, gy % SIDE

    def peer(dz, dy):
        return ((my_z + dz + SIDE) % SIDE) * SIDE + (my_y + dy + SIDE) % SIDE

    owner_of = [gy] + [peer(dz, dy) for dz, dy in OFFSETS]

    table_copy = pltpu.make_async_copy(table_hbm, table_in, local_sem.at[0])
    history_copy = pltpu.make_async_copy(history_hbm, history_in, local_sem.at[1])
    key_copy = pltpu.make_async_copy(w_key_hbm, w_key, local_sem.at[2])
    query_copy = pltpu.make_async_copy(w_query_hbm, w_query, local_sem.at[3])
    out_copy = pltpu.make_async_copy(w_out_hbm, w_out, local_sem.at[4])
    history_copy.start()
    table_copy.start()
    key_copy.start()
    query_copy.start()
    out_copy.start()

    barrier = pltpu.get_barrier_semaphore()
    for dz, dy in OFFSETS:
        pl.semaphore_signal(barrier, inc=1, device_id=(gx, peer(dz, dy)), device_id_type=MESH)
    for d in range(1, members):
        pl.semaphore_signal(
            barrier, inc=1, device_id=((gx + d) % members, gy), device_id_type=MESH
        )

    lane = lax.broadcasted_iota(i32, (128, 128), 1)
    sublane = lax.broadcasted_iota(i32, (128, 128), 0)
    below = (lane < sublane).astype(bf16)
    slot_lane = lax.broadcasted_iota(i32, (128, 2 * 128), 1).astype(f32)
    owner_lane = (lane % groups).astype(f32)
    square[...] = jnp.zeros_like(square)
    for b in range(blocks):
        square[0, b : b + 1, :] = owner_ref[:, b * 128 : (b + 1) * 128].astype(f32)
    owners = square[0].T
    square[1, 0:blocks, :] = (row_ref[...] // 64).astype(f32)
    high = square[1].T
    square[2, 0:blocks, :] = (row_ref[...] % 64).astype(f32)
    low = square[2].T
    carry = jnp.zeros((1, 128), f32)
    parts = jnp.zeros((128, 2 * 128), f32)
    ranks = []
    for b in range(blocks):
        named = owners[:, b : b + 1] == owner_lane
        onehot = jnp.where(named & (lane < groups), 1.0, 0.0)
        prior = jnp.dot(below, onehot.astype(bf16), preferred_element_type=f32) + carry
        carry = carry + jnp.sum(onehot, axis=0, keepdims=True)
        rank = jnp.sum(onehot * prior, axis=1, keepdims=True)
        ranks.append(rank)
        digits = jnp.where(lane < groups, high[:, b : b + 1], low[:, b : b + 1])
        digits = jnp.where(named & (lane < 2 * groups), digits, 0.0)
        chosen = jnp.where(rank == slot_lane, 1.0, 0.0)
        parts = parts + jnp.dot(
            digits.T.astype(bf16), chosen.astype(bf16), preferred_element_type=f32
        )
    rows = (parts[0:groups] * 64.0 + parts[groups : 2 * groups]).astype(i32)
    rows = jnp.clip(rows, 0, table.shape[0] - 1)
    request[:, 0, :] = rows[:, 0:128]
    request[:, 1, :] = rows[:, 128:256]
    counts[...] = jnp.broadcast_to(carry.astype(i32), counts.shape)

    pl.semaphore_wait(barrier, PEERS + members - 1)

    ask = []
    for k in range(PEERS):
        to = owner_of[k + 1]
        ask.append(
            pltpu.make_async_remote_copy(
                request.at[to],
                asked.at[k],
                asked_send.at[k],
                asked_recv.at[k],
                device_id=(gx, to),
                device_id_type=MESH,
            )
        )
        ask[-1].start()
    count_copy = pltpu.make_async_copy(counts, counts_scalar, local_sem.at[5])
    count_copy.start()

    history_copy.wait()
    for l in range(LAYERS):
        for d in range(1, members):
            to = (gx + d) % members
            history_out[l, d] = history_in[l, assign_ref[0, to]]
        here = pl.ds(pl.multiple_of(gx * span, span), span)
        history_all[l, here, :] = history_in[l, assign_ref[0, gx]]

    spread = []
    for l in range(LAYERS):
        for d in range(1, members):
            to = (gx + d) % members
            spread.append(
                pltpu.make_async_remote_copy(
                    history_out.at[l, d],
                    history_all.at[l, pl.ds(pl.multiple_of(gx * span, span), span), :],
                    hist_send.at[l, d],
                    hist_recv.at[l, d],
                    device_id=(to, gy),
                    device_id_type=MESH,
                )
            )
            spread[-1].start()

    table_copy.wait()
    step = 256

    @pl.loop(0, table_in.shape[0] // step)
    def _(t):
        at = pl.ds(pl.multiple_of(t * step, step), step)
        for c in range(width // 128):
            table[at, c, :] = table_in[at, c * 128 : (c + 1) * 128].astype(f32)

    def collect(index, box, slot):
        for part in range(2):
            @pl.loop(0, min(128, capacity - part * 128) // 16)
            def _(t):
                for j in range(16):
                    row = jnp.clip(asked_scalar[index, part, t * 16 + j], 0, table.shape[0] - 1)
                    stage[pl.ds(part * 128 + t * 16 + j, 1)] = table[pl.ds(row, 1)]

        for c in range(width // 128):
            box[slot, :, c * 128 : (c + 1) * 128] = stage[:, c, :].astype(bf16)

    asked[PEERS] = request[gy]
    for k in range(PEERS):
        ask[k].wait_recv()
    scalars = pltpu.make_async_copy(asked, asked_scalar, local_sem.at[6])
    scalars.start()
    scalars.wait()

    def reply(k, dz, dy):
        to = peer(-dz, -dy)
        return pltpu.make_async_remote_copy(
            outbox.at[k],
            inbox.at[k + 1],
            row_send.at[k],
            row_recv.at[k],
            device_id=(gx, to),
            device_id_type=MESH,
        )

    def serve(k, digits):
        z, y, last_z, last_y = digits
        collect(k, outbox, k)

        @pl.when(k > 0)
        def _():
            reply(k - 1, last_z, last_y).start()

        return z // SIDE, y // SIDE, z % SIDE, y % SIDE

    lax.fori_loop(0, PEERS, serve, (PACKED_Z, PACKED_Y, 0, 0))
    reply(PEERS - 1, *OFFSETS[-1]).start()
    collect(PEERS, inbox, 0)

    order_row = jnp.full((128, 128), groups, i32)
    order_column = jnp.full((128, 128), groups, i32)
    for j in range(groups):
        order_row = jnp.where(lane == owner_of[j], j, order_row)
        order_column = jnp.where(sublane == owner_of[j], j, order_column)
    earlier = ((order_column < order_row) & (sublane < groups)).astype(bf16)
    before = jnp.dot(
        jnp.broadcast_to(carry, (8, 128)).astype(bf16), earlier, preferred_element_type=f32
    )[0:1]
    for b in range(blocks):
        onehot = (owners[:, b : b + 1] == owner_lane) & (lane < groups)
        start = jnp.sum(jnp.where(onehot, before, 0.0), axis=1, keepdims=True)
        rank_ref[b * 128 : (b + 1) * 128, :] = jnp.broadcast_to(ranks[b] + start, (128, 128)).astype(i32)
    count_copy.wait()
    found_counts = [counts_scalar[0, owner_of[j]] for j in range(groups)]
    starts = [jnp.int32(0)]
    for j in range(groups - 1):
        starts.append(starts[-1] + found_counts[j])

    four = 4 * capacity
    four_lane = lax.broadcasted_iota(i32, (1, four), 1)

    def put(first):
        target = jnp.full((1, four), -1, i32)
        for j in range(4):
            slot = first + j
            if slot > 0:
                reply(slot - 1, *OFFSETS[slot - 1]).wait_recv()
            at = four_lane - j * capacity
            target = jnp.where(
                (at >= 0) & (at < found_counts[slot]), at + starts[slot], target
            )
        rows = inbox[first : first + 4].reshape(four, width)
        for b in range(2):
            if (first == 0 and b == 1) or (first == 12 and b == 0):
                continue
            row = lax.broadcasted_iota(i32, (half, 128), 0) + b * half
            onehot = jnp.concatenate(
                [
                    jnp.where(row == target[:, c : c + 128], 1.0, 0.0).astype(bf16)
                    for c in range(0, four, 128)
                ],
                axis=1,
            )
            found = jnp.dot(onehot, rows, preferred_element_type=f32)
            if first == 4 * b:
                taken[b] = found
            else:
                taken[b] = taken[b] + found

    live = length_ref[0, assign_ref[0, gx]]

    def project(l):
        for d in range(1, members):
            spread[l * (members - 1) + d - 1].wait_recv()
        size = 512

        @pl.loop(0, history_all.shape[1] // size)
        def _(b):
            at = pl.ds(pl.multiple_of(b * size, size), size)
            normed = rms_scale(history_all[l, at, :].astype(f32), gain_ref[l : l + 1, :])
            both = silu(jnp.dot(normed.astype(bf16), w_key[l], preferred_element_type=f32))
            position = lax.broadcasted_iota(i32, (size, 1), 0) + b * size
            key_value[l, at, 0:width] = both[:, 0:width].astype(bf16)
            key_value[l, at, width : 2 * width] = jnp.where(
                position < live, both[:, width : 2 * width], 0.0
            ).astype(bf16)

    def score(stream):
        head = width // HEADS
        keys = 256
        for l in range(LAYERS):
            normed = rms_scale(stream, gain_ref[l : l + 1, :]).astype(bf16)
            gate_query = silu(jnp.dot(normed, w_query[l], preferred_element_type=f32)).astype(bf16)
            outs = []
            for h in range(HEADS):
                query = gate_query[:, width + h * head : width + (h + 1) * head]
                attended = None
                for k in range(0, key_value.shape[1], keys):
                    scores = lax.dot_general(
                        query,
                        key_value[l, k : k + keys, h * head : (h + 1) * head],
                        (((1,), (1,)), ((), ())),
                        preferred_element_type=f32,
                    )
                    scores = scores * (0.5 * head**-0.5)
                    weights = (scores + scores * jnp.tanh(scores)).astype(bf16)
                    part = jnp.dot(
                        weights,
                        key_value[l, k : k + keys, width + h * head : width + (h + 1) * head],
                        preferred_element_type=f32,
                    )
                    attended = part if attended is None else attended + part
                outs.append(attended)
            gated = rms_scale(jnp.concatenate(outs, axis=1), attn_ref[l : l + 1, :])
            gated = gated * gate_query[:, :width].astype(f32)
            stream = stream + jnp.dot(gated.astype(bf16), w_out[l], preferred_element_type=f32)
        return stream

    put(0)
    key_copy.wait()
    project(0)
    put(4)
    project(1)
    query_copy.wait()
    out_copy.wait()
    put(8)

    @pl.loop(0, 2)
    def _(b):
        @pl.when(b == 1)
        def _():
            put(12)

        scored = score(taken[b]).astype(bf16)

        @pl.loop(0, 2)
        def _(part):
            at = pl.ds(pl.multiple_of(part * half, half), half)
            rank = rank_ref[at, :]
            onehot = jnp.concatenate(
                [
                    jnp.where(rank == lane[0:1] + (c + b * half), 1.0, 0.0).astype(bf16)
                    for c in range(0, half, 128)
                ],
                axis=1,
            )
            found = jnp.dot(onehot, scored, preferred_element_type=f32)

            @pl.when(b == 0)
            def _():
                total[at, :] = found

            @pl.when(b == 1)
            def _():
                out_ref[at, :] = (total[at, :] + found).astype(bf16)

    for k in range(PEERS):
        ask[k].wait_send()
        reply(k, *OFFSETS[k]).wait_send()
    for copy in spread:
        copy.wait_send()


VMEM = pl.BlockSpec(memory_space=pltpu.VMEM)
SMEM = pl.BlockSpec(memory_space=pltpu.SMEM)
ANY = pl.BlockSpec(memory_space=pl.ANY)


def local(
    table,
    history,
    lengths,
    assignment,
    cand_owner,
    cand_row,
    norm_gain,
    w_query,
    w_key,
    attn_gain,
    w_out,
):
    groups = lax.axis_size("gy")
    members = lax.axis_size("gx")
    count = cand_row.shape[0]
    rows, width = table.shape
    span = history.shape[2]
    capacity = 2 * count // groups
    dma = pltpu.SemaphoreType.DMA
    vmem = pltpu.VMEM
    return pl.pallas_call(
        functools.partial(program_kernel, capacity),
        out_shape=jax.ShapeDtypeStruct((count, width), bf16),
        in_specs=[VMEM, VMEM, VMEM, VMEM, SMEM, SMEM, ANY, ANY, ANY, ANY, ANY],
        out_specs=VMEM,
        scratch_shapes=[
            vmem((3, 128, 128), f32),
            vmem((8, 128), i32),
            pltpu.SMEM((8, 128), i32),
            vmem((count, 128), i32),
            vmem((rows, width), bf16),
            vmem((rows, width // 128, 128), f32),
            vmem((groups, 2, 128), i32),
            vmem((groups, 2, 128), i32),
            pltpu.SMEM((groups, 2, 128), i32),
            vmem((capacity, width // 128, 128), f32),
            vmem((PEERS, capacity, width), bf16),
            vmem((groups, capacity, width), bf16),
            vmem((2, count // 2, width), f32),
            vmem((count, width), f32),
            vmem(history.shape, bf16),
            vmem((LAYERS, members, span, width), bf16),
            vmem((LAYERS, members * span, width), bf16),
            vmem((LAYERS, members * span, 2 * width), bf16),
            vmem(w_key.shape, bf16),
            vmem(w_query.shape, bf16),
            vmem(w_out.shape, bf16),
            dma((7,)),
            dma((PEERS,)),
            dma((PEERS,)),
            dma((PEERS,)),
            dma((PEERS,)),
            dma((LAYERS, members)),
            dma((LAYERS, members)),
        ],
        compiler_params=pltpu.CompilerParams(
            collective_id=0, has_side_effects=True, vmem_limit_bytes=62 << 20
        ),
        name="hstu",
    )(
        cand_owner.T,
        cand_row.reshape(count // 128, 128),
        norm_gain,
        attn_gain,
        assignment,
        lengths,
        table,
        history,
        w_key,
        w_query,
        w_out,
    )


def solution(mesh):
    both = ("gx", "gy")
    return jax.shard_map(
        local,
        mesh=mesh,
        in_specs=(
            P("gy", None),
            P(None, "gy", "gx", None),
            P("gy", None),
            P("gy", None),
            P(both, None),
            P(both),
            P(),
            P(),
            P(),
            P(),
            P(),
        ),
        out_specs=P(both, None),
        check_vma=False,
    )
```

```python
import functools

import jax
import jax.numpy as jnp
from jax import lax
from jax.experimental import pallas as pl
from jax.experimental.pallas import tpu as pltpu
from jax.sharding import PartitionSpec as P

HEADS = 4
LAYERS = 2
EPSILON = 1e-06
MESH = pl.DeviceIdType.MESH
f32, bf16, i32 = jnp.float32, jnp.bfloat16, jnp.int32

OFFSETS = (
    (0, 1), (1, 0), (0, 3), (3, 0), (1, 1), (3, 3), (1, 3), (3, 1),
    (0, 2), (2, 0), (2, 1), (1, 2), (2, 3), (3, 2), (2, 2),
)
SIDE = 4
PEERS = len(OFFSETS)
PACKED_Z = sum(z * SIDE**k for k, (z, _) in enumerate(OFFSETS))
PACKED_Y = sum(y * SIDE**k for k, (_, y) in enumerate(OFFSETS))


def silu(v):
    half = v * 0.5
    return half + half * jnp.tanh(half)


def rms_scale(vector, gain_row):
    return vector * lax.rsqrt(jnp.mean(vector * vector, axis=-1, keepdims=True) + EPSILON) * gain_row


def program_kernel(
    capacity,
    owner_ref,
    row_ref,
    gain_ref,
    attn_ref,
    assign_ref,
    length_ref,
    table_hbm,
    history_hbm,
    w_key_hbm,
    w_query_hbm,
    w_out_hbm,
    out_ref,
    square,
    counts,
    counts_scalar,
    rank_ref,
    table_in,
    table,
    request,
    asked,
    asked_scalar,
    stage,
    outbox,
    inbox,
    taken,
    total,
    history_in,
    history_out,
    history_all,
    key_value,
    w_key,
    w_query,
    w_out,
    local_sem,
    asked_send,
    asked_recv,
    row_send,
    row_recv,
    hist_send,
    hist_recv,
):
    count, width = out_ref.shape
    half = count // 2
    blocks = count // 128
    groups = lax.axis_size("gy")
    members = lax.axis_size("gx")
    span = history_in.shape[2]
    gx = lax.axis_index("gx")
    gy = lax.axis_index("gy")
    my_z, my_y = gy // SIDE, gy % SIDE

    def peer(dz, dy):
        return ((my_z + dz + SIDE) % SIDE) * SIDE + (my_y + dy + SIDE) % SIDE

    owner_of = [gy] + [peer(dz, dy) for dz, dy in OFFSETS]

    table_copy = pltpu.make_async_copy(table_hbm, table_in, local_sem.at[0])
    history_copy = pltpu.make_async_copy(history_hbm, history_in, local_sem.at[1])
    key_copy = pltpu.make_async_copy(w_key_hbm, w_key, local_sem.at[2])
    query_copy = pltpu.make_async_copy(w_query_hbm, w_query, local_sem.at[3])
    out_copy = pltpu.make_async_copy(w_out_hbm, w_out, local_sem.at[4])
    history_copy.start()
    table_copy.start()
    key_copy.start()
    query_copy.start()
    out_copy.start()

    barrier = pltpu.get_barrier_semaphore()
    for dz, dy in OFFSETS:
        pl.semaphore_signal(barrier, inc=1, device_id=(gx, peer(dz, dy)), device_id_type=MESH)
    for d in range(1, members):
        pl.semaphore_signal(
            barrier, inc=1, device_id=((gx + d) % members, gy), device_id_type=MESH
        )

    lane = lax.broadcasted_iota(i32, (128, 128), 1)
    sublane = lax.broadcasted_iota(i32, (128, 128), 0)
    below = (lane < sublane).astype(bf16)
    slot_lane = lax.broadcasted_iota(i32, (128, 2 * 128), 1).astype(f32)
    owner_lane = (lane % groups).astype(f32)
    square[...] = jnp.zeros_like(square)
    for b in range(blocks):
        square[0, b : b + 1, :] = owner_ref[:, b * 128 : (b + 1) * 128].astype(f32)
    owners = square[0].T
    square[1, 0:blocks, :] = (row_ref[...] // 64).astype(f32)
    high = square[1].T
    square[2, 0:blocks, :] = (row_ref[...] % 64).astype(f32)
    low = square[2].T
    carry = jnp.zeros((1, 128), f32)
    parts = jnp.zeros((128, 2 * 128), f32)
    ranks = []
    for b in range(blocks):
        named = owners[:, b : b + 1] == owner_lane
        onehot = jnp.where(named & (lane < groups), 1.0, 0.0)
        prior = jnp.dot(below, onehot.astype(bf16), preferred_element_type=f32) + carry
        carry = carry + jnp.sum(onehot, axis=0, keepdims=True)
        rank = jnp.sum(onehot * prior, axis=1, keepdims=True)
        ranks.append(rank)
        digits = jnp.where(lane < groups, high[:, b : b + 1], low[:, b : b + 1])
        digits = jnp.where(named & (lane < 2 * groups), digits, 0.0)
        chosen = jnp.where(rank == slot_lane, 1.0, 0.0)
        parts = parts + jnp.dot(
            digits.T.astype(bf16), chosen.astype(bf16), preferred_element_type=f32
        )
    rows = (parts[0:groups] * 64.0 + parts[groups : 2 * groups]).astype(i32)
    rows = jnp.clip(rows, 0, table.shape[0] - 1)
    request[:, 0, :] = rows[:, 0:128]
    request[:, 1, :] = rows[:, 128:256]
    counts[...] = jnp.broadcast_to(carry.astype(i32), counts.shape)

    pl.semaphore_wait(barrier, PEERS + members - 1)

    ask = []
    for k in range(PEERS):
        to = owner_of[k + 1]
        ask.append(
            pltpu.make_async_remote_copy(
                request.at[to],
                asked.at[k],
                asked_send.at[k],
                asked_recv.at[k],
                device_id=(gx, to),
                device_id_type=MESH,
            )
        )
        ask[-1].start()
    count_copy = pltpu.make_async_copy(counts, counts_scalar, local_sem.at[5])
    count_copy.start()

    history_copy.wait()
    for l in range(LAYERS):
        for d in range(1, members):
            to = (gx + d) % members
            history_out[l, d] = history_in[l, assign_ref[0, to]]
        here = pl.ds(pl.multiple_of(gx * span, span), span)
        history_all[l, here, :] = history_in[l, assign_ref[0, gx]]

    spread = []
    for l in range(LAYERS):
        for d in range(1, members):
            to = (gx + d) % members
            spread.append(
                pltpu.make_async_remote_copy(
                    history_out.at[l, d],
                    history_all.at[l, pl.ds(pl.multiple_of(gx * span, span), span), :],
                    hist_send.at[l, d],
                    hist_recv.at[l, d],
                    device_id=(to, gy),
                    device_id_type=MESH,
                )
            )
            spread[-1].start()

    table_copy.wait()
    step = 256

    @pl.loop(0, table_in.shape[0] // step)
    def _(t):
        at = pl.ds(pl.multiple_of(t * step, step), step)
        table[at, :] = table_in[at, :].astype(f32)

    def collect(index, box, slot):
        for part in range(2):
            @pl.loop(0, min(128, capacity - part * 128) // 16)
            def _(t):
                for j in range(16):
                    row = jnp.clip(asked_scalar[index, part, t * 16 + j], 0, table.shape[0] - 1)
                    stage[pl.ds(part * 128 + t * 16 + j, 1), :] = table[pl.ds(row, 1), :]

        box[slot] = stage[...].astype(bf16)

    asked[PEERS] = request[gy]
    for k in range(PEERS):
        ask[k].wait_recv()
    scalars = pltpu.make_async_copy(asked, asked_scalar, local_sem.at[6])
    scalars.start()
    scalars.wait()

    def reply(k, dz, dy):
        to = peer(-dz, -dy)
        return pltpu.make_async_remote_copy(
            outbox.at[k],
            inbox.at[k + 1],
            row_send.at[k],
            row_recv.at[k],
            device_id=(gx, to),
            device_id_type=MESH,
        )

    def serve(k, digits):
        z, y, last_z, last_y = digits
        collect(k, outbox, k)

        @pl.when(k > 0)
        def _():
            reply(k - 1, last_z, last_y).start()

        return z // SIDE, y // SIDE, z % SIDE, y % SIDE

    lax.fori_loop(0, PEERS, serve, (PACKED_Z, PACKED_Y, 0, 0))
    reply(PEERS - 1, *OFFSETS[-1]).start()
    collect(PEERS, inbox, 0)

    order_row = jnp.full((128, 128), groups, i32)
    order_column = jnp.full((128, 128), groups, i32)
    for j in range(groups):
        order_row = jnp.where(lane == owner_of[j], j, order_row)
        order_column = jnp.where(sublane == owner_of[j], j, order_column)
    earlier = ((order_column < order_row) & (sublane < groups)).astype(bf16)
    before = jnp.dot(
        jnp.broadcast_to(carry, (8, 128)).astype(bf16), earlier, preferred_element_type=f32
    )[0:1]
    for b in range(blocks):
        onehot = (owners[:, b : b + 1] == owner_lane) & (lane < groups)
        start = jnp.sum(jnp.where(onehot, before, 0.0), axis=1, keepdims=True)
        rank_ref[b * 128 : (b + 1) * 128, :] = jnp.broadcast_to(ranks[b] + start, (128, 128)).astype(i32)
    count_copy.wait()
    found_counts = [counts_scalar[0, owner_of[j]] for j in range(groups)]
    starts = [jnp.int32(0)]
    for j in range(groups - 1):
        starts.append(starts[-1] + found_counts[j])

    four = 4 * capacity
    four_lane = lax.broadcasted_iota(i32, (1, four), 1)

    def put(first):
        target = jnp.full((1, four), -1, i32)
        for j in range(4):
            slot = first + j
            if slot > 0:
                reply(slot - 1, *OFFSETS[slot - 1]).wait_recv()
            at = four_lane - j * capacity
            target = jnp.where(
                (at >= 0) & (at < found_counts[slot]), at + starts[slot], target
            )
        rows = inbox[first : first + 4].reshape(four, width)
        for b in range(2):
            if (first == 0 and b == 1) or (first == 12 and b == 0):
                continue
            row = lax.broadcasted_iota(i32, (half, 128), 0) + b * half
            onehot = jnp.concatenate(
                [
                    jnp.where(row == target[:, c : c + 128], 1.0, 0.0).astype(bf16)
                    for c in range(0, four, 128)
                ],
                axis=1,
            )
            found = jnp.dot(onehot, rows, preferred_element_type=f32)
            if first == 4 * b:
                taken[b] = found
            else:
                taken[b] = taken[b] + found

    live = length_ref[0, assign_ref[0, gx]]

    def project(l):
        for d in range(1, members):
            spread[l * (members - 1) + d - 1].wait_recv()
        size = 512

        @pl.loop(0, history_all.shape[1] // size)
        def _(b):
            at = pl.ds(pl.multiple_of(b * size, size), size)
            normed = rms_scale(history_all[l, at, :].astype(f32), gain_ref[l : l + 1, :])
            both = silu(jnp.dot(normed.astype(bf16), w_key[l], preferred_element_type=f32))
            position = lax.broadcasted_iota(i32, (size, 1), 0) + b * size
            key_value[l, at, 0:width] = both[:, 0:width].astype(bf16)
            key_value[l, at, width : 2 * width] = jnp.where(
                position < live, both[:, width : 2 * width], 0.0
            ).astype(bf16)

    def score(stream):
        head = width // HEADS
        keys = 256
        for l in range(LAYERS):
            normed = rms_scale(stream, gain_ref[l : l + 1, :]).astype(bf16)
            gate_query = silu(jnp.dot(normed, w_query[l], preferred_element_type=f32)).astype(bf16)
            outs = []
            for h in range(HEADS):
                query = gate_query[:, width + h * head : width + (h + 1) * head]
                attended = None
                for k in range(0, key_value.shape[1], keys):
                    scores = lax.dot_general(
                        query,
                        key_value[l, k : k + keys, h * head : (h + 1) * head],
                        (((1,), (1,)), ((), ())),
                        preferred_element_type=f32,
                    )
                    scores = scores * (0.5 * head**-0.5)
                    weights = (scores + scores * jnp.tanh(scores)).astype(bf16)
                    part = jnp.dot(
                        weights,
                        key_value[l, k : k + keys, width + h * head : width + (h + 1) * head],
                        preferred_element_type=f32,
                    )
                    attended = part if attended is None else attended + part
                outs.append(attended)
            gated = rms_scale(jnp.concatenate(outs, axis=1), attn_ref[l : l + 1, :])
            gated = gated * gate_query[:, :width].astype(f32)
            stream = stream + jnp.dot(gated.astype(bf16), w_out[l], preferred_element_type=f32)
        return stream

    put(0)
    key_copy.wait()
    project(0)
    put(4)
    project(1)
    query_copy.wait()
    out_copy.wait()
    put(8)

    @pl.loop(0, 2)
    def _(b):
        @pl.when(b == 1)
        def _():
            put(12)

        scored = score(taken[b]).astype(bf16)

        @pl.loop(0, 2)
        def _(part):
            at = pl.ds(pl.multiple_of(part * half, half), half)
            rank = rank_ref[at, :]
            onehot = jnp.concatenate(
                [
                    jnp.where(rank == lane[0:1] + (c + b * half), 1.0, 0.0).astype(bf16)
                    for c in range(0, half, 128)
                ],
                axis=1,
            )
            found = jnp.dot(onehot, scored, preferred_element_type=f32)

            @pl.when(b == 0)
            def _():
                total[at, :] = found

            @pl.when(b == 1)
            def _():
                out_ref[at, :] = (total[at, :] + found).astype(bf16)

    for k in range(PEERS):
        ask[k].wait_send()
        reply(k, *OFFSETS[k]).wait_send()
    for copy in spread:
        copy.wait_send()


VMEM = pl.BlockSpec(memory_space=pltpu.VMEM)
SMEM = pl.BlockSpec(memory_space=pltpu.SMEM)
ANY = pl.BlockSpec(memory_space=pl.ANY)


def local(
    table,
    history,
    lengths,
    assignment,
    cand_owner,
    cand_row,
    norm_gain,
    w_query,
    w_key,
    attn_gain,
    w_out,
):
    groups = lax.axis_size("gy")
    members = lax.axis_size("gx")
    count = cand_row.shape[0]
    rows, width = table.shape
    span = history.shape[2]
    capacity = 2 * count // groups
    dma = pltpu.SemaphoreType.DMA
    vmem = pltpu.VMEM
    return pl.pallas_call(
        functools.partial(program_kernel, capacity),
        out_shape=jax.ShapeDtypeStruct((count, width), bf16),
        in_specs=[VMEM, VMEM, VMEM, VMEM, SMEM, SMEM, ANY, ANY, ANY, ANY, ANY],
        out_specs=VMEM,
        scratch_shapes=[
            vmem((3, 128, 128), f32),
            vmem((8, 128), i32),
            pltpu.SMEM((8, 128), i32),
            vmem((count, 128), i32),
            vmem((rows, width), bf16),
            vmem((rows, width), f32),
            vmem((groups, 2, 128), i32),
            vmem((groups, 2, 128), i32),
            pltpu.SMEM((groups, 2, 128), i32),
            vmem((capacity, width), f32),
            vmem((PEERS, capacity, width), bf16),
            vmem((groups, capacity, width), bf16),
            vmem((2, count // 2, width), f32),
            vmem((count, width), f32),
            vmem(history.shape, bf16),
            vmem((LAYERS, members, span, width), bf16),
            vmem((LAYERS, members * span, width), bf16),
            vmem((LAYERS, members * span, 2 * width), bf16),
            vmem(w_key.shape, bf16),
            vmem(w_query.shape, bf16),
            vmem(w_out.shape, bf16),
            dma((7,)),
            dma((PEERS,)),
            dma((PEERS,)),
            dma((PEERS,)),
            dma((PEERS,)),
            dma((LAYERS, members)),
            dma((LAYERS, members)),
        ],
        compiler_params=pltpu.CompilerParams(
            collective_id=0, has_side_effects=True, vmem_limit_bytes=62 << 20
        ),
        name="hstu",
    )(
        cand_owner.T,
        cand_row.reshape(count // 128, 128),
        norm_gain,
        attn_gain,
        assignment,
        lengths,
        table,
        history,
        w_key,
        w_query,
        w_out,
    )


def solution(mesh):
    both = ("gx", "gy")
    return jax.shard_map(
        local,
        mesh=mesh,
        in_specs=(
            P("gy", None),
            P(None, "gy", "gx", None),
            P("gy", None),
            P("gy", None),
            P(both, None),
            P(both),
            P(),
            P(),
            P(),
            P(),
            P(),
        ),
        out_specs=P(both, None),
        check_vma=False,
    )
```
